32 devices in a mesh: groups: 2 (over y), seq: 4 (over z), adapt: 4 (over x, core).
Axes of the slice: x: 2, y: 2, z: 4, core: 2. Of those that a mesh axis runs over, the one named last changes fastest.
Arguments:
- image: bfloat16 [16, 2048, 3072], P(('groups', 'adapt'), 'seq'), parts along dimension 0, may hold values from -6 to 6
- modulation: float32 [16, 2, 3072], P(('groups', 'adapt')), parts along dimension 0, may hold values from -3 to 3
- query_key_value_weight: bfloat16 [3072, 6144], P(None, 'adapt'), may hold values from -0.109375 to 0.109375
- pooled_down_factor: bfloat16 [16, 3072, 64], P('seq'), may hold values from -0.109375 to 0.109375
- pooled_up_factor: bfloat16 [16, 64, 6144], P('seq', None, 'adapt'), may hold values from -0.75 to 0.75
- request_adapter: int32 [16], P('groups'), parts along dimension 0, may hold values from 0 to 15
- adapter_slot_table: int32 [16], replicated, may hold values from 0 to 15, each once
- row_request: int32 [16], P('groups'), parts along dimension 0, may hold values from 0 to 7, each once
- text_key_value: bfloat16 [16, 512, 2, 2048], P('groups', 'seq', None, 'adapt'), parts along dimension 0, may hold values from -110 to 110
- query_key_gain: float32 [2, 128], replicated, may hold values from 1 to 2.5
Outputs:
- attended: bfloat16 [16, 2048, 2048], P('groups', 'seq', 'adapt'), parts along dimension 0
The draws below stay inside these ranges and needn't reach their ends.
There are 2 independent parts, one for each index of `groups`. The reference program is written for one: setup_inputs(seed, part) draws one part's arguments, and reference() takes and returns one part's arrays. A program takes and returns all parts, laid end to end along the dimension named above; an argument that names none is the same for every part. Nothing has to cross between parts.
All inputs are finite; a program needn't handle non-finite values.
Results may differ from the reference program's by a relative error of at most 0.0049.
The reference program's roundings to bfloat16 on the way (of `modulated`, `shrunk` and `probs`) count: a program that leaves them out, or rounds other values in their place, can miss the bound.
Values may be sent and summed in bfloat16 or wider, within the bound.
A program may use at most 192 MiB of HBM per device.

```python
import math
import jax
import jax.numpy as jnp
import numpy as np
from jax import lax

MODEL_WIDTH = 3072
HEAD_SIZE = 128
LOCAL_HEADS = 16
ADAPTER_RANK = 64
IMG = 2048
TXT = 512
REQS = 8
ADAPTER_POOL = 16


def draw_text_key_value(key, part):
    first = jax.random.fold_in(key, 0)
    array_shape = (REQS, TXT, 2, LOCAL_HEADS * HEAD_SIZE)
    return jnp.clip(jax.random.normal(first, array_shape, jnp.float32), -6.0, 6.0).astype(jnp.bfloat16)


def place_ends(drawn, key, low, high):
    dims = drawn.shape
    index_at = [jax.random.randint(jax.random.fold_in(key, axis), (), 0, dims[axis]) for axis in range(len(dims))]
    drawn = drawn.at[tuple(index_at)].set(low)
    longest = dims.index(max(dims))
    index_at[longest] = (index_at[longest] + 1) % dims[longest]
    return drawn.at[tuple(index_at)].set(high)


def level_of(key, extent, cuts, least, high):
    loudness, own = 1.0, jax.random.fold_in(key, 6)
    for axis_at, blocks in cuts:
        draws = jnp.exp(jax.random.uniform(jax.random.fold_in(own, axis_at), (blocks,), jnp.float32, least / len(cuts), high / len(cuts)))
        loudness = loudness * jnp.repeat(draws, extent[axis_at] // blocks).reshape([-1 if axis == axis_at else 1 for axis in range(len(extent))])
    return loudness


def rank_table(amount, lean):
    weights = [(1 << 20) // math.isqrt(grade ** lean) + 1 for grade in range(1, amount + 1)]
    width = 1 + sum(weights) // (1 << 30)
    return np.cumsum(np.array([max(1, weight // width) for weight in weights]))


def ranked(stream_key, extent, count, slope):
    listing = rank_table(count, slope)
    ticket = jax.random.randint(jax.random.fold_in(stream_key, 1), extent, 0, int(listing[count - 1]))
    grade = jnp.searchsorted(jnp.asarray(listing, jnp.int32), ticket, side="right")
    return jax.random.permutation(jax.random.fold_in(stream_key, 2), count)[grade].astype(jnp.int32)


def scatter_about(key, dims, spread, most, cuts=(), held_as=jnp.bfloat16):
    values = jax.random.normal(key, dims, jnp.float32) * spread
    if len(cuts) > 0:
        values = level_of(key, dims, cuts, -0.22, 0.18) * values
    return jnp.clip(values, min=-most, max=most).astype(held_as)


def setup_inputs(seed: int = 0, part: int = 0) -> dict:
    streams_of = jax.random.split(jax.random.key(seed), 11)
    part_keys = jax.random.split(jax.random.fold_in(streams_of[10], part), 11)
    image = scatter_about(part_keys[0], (REQS, IMG, MODEL_WIDTH), 1.0, 6.0, ((0, 4), (1, 4)))
    modulation = scatter_about(part_keys[1], (REQS, 2, MODEL_WIDTH), 0.5, 3.0, ((0, 4),), jnp.float32)
    query_key_value_weight = scatter_about(streams_of[2], (MODEL_WIDTH, 3 * LOCAL_HEADS * HEAD_SIZE), MODEL_WIDTH ** -0.5, 0.109375, ((1, 4),))
    pooled_down_factor = scatter_about(streams_of[3], (ADAPTER_POOL, MODEL_WIDTH, ADAPTER_RANK), MODEL_WIDTH ** -0.5, 0.109375, ((0, 4),))
    pooled_up_factor = scatter_about(streams_of[4], (ADAPTER_POOL, ADAPTER_RANK, 3 * LOCAL_HEADS * HEAD_SIZE), ADAPTER_RANK ** -0.5, 0.75, ((0, 4), (2, 4)))
    request_adapter = place_ends(ranked(part_keys[5], (REQS,), ADAPTER_POOL, 2), jax.random.fold_in(part_keys[5], 3), 0, ADAPTER_POOL - 1).astype(jnp.int32)
    adapter_slot_table = jax.random.permutation(streams_of[6], ADAPTER_POOL).astype(jnp.int32)
    row_request = jax.random.permutation(part_keys[7], REQS).astype(jnp.int32)
    text_key_value = draw_text_key_value(jax.random.fold_in(jax.random.fold_in(streams_of[10], part), 71), part)
    query_key_gain = jnp.clip(jnp.exp(jax.random.uniform(streams_of[9], (2, HEAD_SIZE), jnp.float32, math.log(1.0), math.log(2.5))), 1.0, 2.5)
    return {"image": image, "modulation": modulation, "query_key_value_weight": query_key_value_weight, "pooled_down_factor": pooled_down_factor, "pooled_up_factor": pooled_up_factor, "request_adapter": request_adapter, "adapter_slot_table": adapter_slot_table, "row_request": row_request, "text_key_value": text_key_value, "query_key_gain": query_key_gain}


def rms_scale(values, gain):
    return values * lax.rsqrt(lax.optimization_barrier(jnp.mean(values * values, axis=-1, keepdims=True)) + 1e-06) * gain

def reference(image, modulation, query_key_value_weight, pooled_down_factor, pooled_up_factor, request_adapter, adapter_slot_table, row_request, text_key_value, query_key_gain):
    widened = image.astype(jnp.float32)
    centre = widened - lax.optimization_barrier(jnp.mean(widened, axis=-1, keepdims=True))
    variance = lax.optimization_barrier(jnp.mean(centre * centre, axis=-1, keepdims=True))
    normed = centre * lax.rsqrt(variance + 1e-06)
    modulated = ((1.0 + modulation[:, 1, None, :]) * normed + modulation[:, 0, None, :]).astype(jnp.bfloat16)
    slots = adapter_slot_table[request_adapter[row_request]].astype(jnp.int32)
    inverse = 1.0 / HEAD_SIZE ** 0.5

    def per_head(operands):
        head_q, head_k, head_v = operands
        scores = jnp.einsum('qd,kd->qk', head_q.astype(jnp.float32), head_k.astype(jnp.float32)) * inverse
        probs = jax.nn.softmax(scores, axis=-1).astype(jnp.bfloat16)
        return jnp.dot(probs, head_v, preferred_element_type=jnp.float32).astype(jnp.bfloat16)

    def per_request(operands):
        token_rows, storage_slot, text_part = operands
        down_factor = pooled_down_factor[storage_slot]
        up_factor = pooled_up_factor[storage_slot]
        shrunk = jnp.dot(token_rows, down_factor, preferred_element_type=jnp.float32).astype(jnp.bfloat16)
        qkv = jnp.dot(token_rows, query_key_value_weight, preferred_element_type=jnp.float32)
        qkv = qkv + jnp.dot(shrunk, up_factor, preferred_element_type=jnp.float32)
        qkv = qkv.reshape(IMG, LOCAL_HEADS, 3, HEAD_SIZE)
        queries = rms_scale(qkv[:, :, 0], query_key_gain[0]).astype(jnp.bfloat16)
        image_keys = rms_scale(qkv[:, :, 1], query_key_gain[1]).astype(jnp.bfloat16)
        image_values = qkv[:, :, 2].astype(jnp.bfloat16)
        text_keys = text_part[:, 0].reshape(TXT, LOCAL_HEADS, HEAD_SIZE)
        text_values = text_part[:, 1].reshape(TXT, LOCAL_HEADS, HEAD_SIZE)
        all_keys = jnp.concatenate([image_keys, text_keys], axis=0)
        all_values = jnp.concatenate([image_values, text_values], axis=0)
        outputs = lax.map(per_head, (jnp.transpose(queries, (1, 0, 2)), jnp.transpose(all_keys, (1, 0, 2)), jnp.transpose(all_values, (1, 0, 2))))
        return jnp.transpose(outputs, (1, 0, 2)).reshape(IMG, LOCAL_HEADS * HEAD_SIZE)
    return lax.map(per_request, (modulated, slots, text_key_value))
```

```python
import functools
import math

import jax
import jax.numpy as jnp
from jax import lax
from jax.experimental import pallas as pl
from jax.experimental.pallas import tpu as pltpu
from jax.sharding import PartitionSpec as P

HEAD_SIZE = 128


def layer_modulate(image, modulation):
    widened = image.astype(jnp.float32)
    centre = widened - jnp.mean(widened, axis=-1, keepdims=True)
    variance = jnp.mean(centre * centre, axis=-1, keepdims=True)
    normed = centre * lax.rsqrt(variance + 1e-06)
    return ((1.0 + modulation[:, 1, None, :]) * normed + modulation[:, 0, None, :]).astype(
        jnp.bfloat16
    )


def rms_scale(values, gain):
    return values * lax.rsqrt(jnp.mean(values * values, axis=-1, keepdims=True) + 1e-06) * gain


def attend_item(operands):
    queries, joined = operands
    key_rows = joined[:, 0]
    value_rows = joined[:, 1]
    query_count = queries.shape[0]
    block = math.gcd(query_count, 512)
    inverse = 1.0 / math.sqrt(queries.shape[-1])
    blocked = queries.reshape(query_count // block, block, queries.shape[-1])

    def one_block(block_rows):
        scores = (
            lax.dot_general(
                block_rows, key_rows, (((1,), (1,)), ((), ())), preferred_element_type=jnp.float32
            )
            * inverse
        )
        highest = jnp.max(scores, axis=-1, keepdims=True)
        weights = jnp.exp(scores - highest)
        weights = weights / jnp.sum(weights, axis=-1, keepdims=True)
        return jnp.dot(
            weights.astype(jnp.bfloat16), value_rows, preferred_element_type=jnp.float32
        ).astype(jnp.bfloat16)

    return lax.map(one_block, blocked).reshape(queries.shape)


def general_device(
    image,
    modulation,
    query_key_value_weight,
    pooled_down_factor,
    pooled_up_factor,
    request_adapter,
    adapter_slot_table,
    row_request,
    text_key_value,
    query_key_gain,
):
    seq_index = lax.axis_index("seq")
    all_requests = request_adapter.shape[0]
    local_pool_slice = pooled_down_factor.shape[0]
    pool_total = adapter_slot_table.shape[0]
    heads_local = query_key_value_weight.shape[1] // (3 * HEAD_SIZE)
    text_local = text_key_value.shape[1]
    modulated = layer_modulate(image, modulation)
    request_match = row_request[:, None] == jnp.arange(all_requests, dtype=jnp.int32)[None, :]
    chosen_ids = jnp.sum(jnp.where(request_match, request_adapter[None, :], 0), axis=1)
    slot_match = chosen_ids[:, None] == jnp.arange(pool_total, dtype=jnp.int32)[None, :]
    slots = jnp.sum(jnp.where(slot_match, adapter_slot_table[None, :], 0), axis=1)
    owned = slots // local_pool_slice == seq_index
    local_match = (slots % local_pool_slice)[:, None] == jnp.arange(
        local_pool_slice, dtype=jnp.int32
    )[None, :]
    slot_picker = (owned[:, None] & local_match).astype(jnp.bfloat16)
    up_terms = jnp.einsum(
        "eq,qfx->efx", slot_picker, pooled_up_factor, preferred_element_type=jnp.float32
    ).astype(jnp.bfloat16)
    down_terms = jnp.einsum(
        "mv,vna->mna", slot_picker, pooled_down_factor, preferred_element_type=jnp.float32
    ).astype(jnp.bfloat16)
    down_fetched, up_fetched = (
        lax.psum(down_terms, "seq").astype(jnp.float32),
        lax.psum(up_terms, "seq").astype(jnp.float32),
    )
    down_fetched = down_fetched.astype(jnp.bfloat16)
    up_fetched = up_fetched.astype(jnp.bfloat16)
    block_rows = lax.all_gather(modulated, "adapt", axis=0, tiled=True)
    shrunk = jnp.einsum(
        "rtd,rdk->rtk", block_rows, down_fetched, preferred_element_type=jnp.float32
    ).astype(jnp.bfloat16)
    frozen = jnp.einsum(
        "rtd,dc->rtc", block_rows, query_key_value_weight, preferred_element_type=jnp.float32
    )
    qkv = frozen + jnp.einsum(
        "rtk,rkc->rtc", shrunk, up_fetched, preferred_element_type=jnp.float32
    )
    token_local = qkv.shape[1]
    qkv = qkv.reshape(all_requests, token_local, heads_local, 3, HEAD_SIZE)
    queries = rms_scale(qkv[:, :, :, 0], query_key_gain[0]).astype(jnp.bfloat16)
    image_keys = rms_scale(qkv[:, :, :, 1], query_key_gain[1]).astype(jnp.bfloat16)
    image_values = qkv[:, :, :, 2].astype(jnp.bfloat16)
    image_pairs = jnp.transpose(jnp.stack([image_keys, image_values], axis=3), (0, 2, 1, 3, 4))
    text_pairs = jnp.transpose(
        text_key_value.reshape(all_requests, text_local, 2, heads_local, HEAD_SIZE), (0, 3, 1, 2, 4)
    )
    joined = jnp.concatenate([image_pairs, text_pairs], axis=2)
    joined = joined.reshape(all_requests * heads_local, token_local + text_local, 2, HEAD_SIZE)
    queries = jnp.transpose(queries, (0, 2, 1, 3)).reshape(
        all_requests * heads_local, token_local, HEAD_SIZE
    )
    query_items, joined_items = (
        lax.all_to_all(queries, "seq", split_axis=0, concat_axis=1, tiled=True),
        lax.all_to_all(joined, "seq", split_axis=0, concat_axis=1, tiled=True),
    )
    attended = lax.map(attend_item, (query_items, joined_items))
    returned = lax.all_to_all(attended, "seq", split_axis=1, concat_axis=0, tiled=True)
    returned = returned.reshape(all_requests, heads_local, token_local, HEAD_SIZE)
    return jnp.transpose(returned, (0, 2, 1, 3)).reshape(
        all_requests, token_local, heads_local * HEAD_SIZE
    )


BF16 = jnp.bfloat16
F32 = jnp.float32
ANY = pl.BlockSpec(memory_space=pl.ANY)


def flipped(index, k):
    low = 1 - 2 * lax.rem(index, 2) if k % 2 else 0
    high = 2 - 4 * (index // 2) if k // 2 else 0
    return index + low + high


def move_kernel(
    mod, text, down, up, tok, txt, down_all, up_all,
    tok_send, tok_recv, side_send, side_recv, across_send, across_recv, last_send, last_recv,
    text_send, text_recv, up_send, up_recv, down_send, down_recv, spread_send, spread_recv,
):
    s = lax.axis_index("seq")
    a = lax.axis_index("adapt")
    x = a // 2
    c = lax.rem(a, 2)
    me = s * 4 + a
    sibling = {"seq": s, "adapt": 2 * x + 1 - c}
    partner = {"seq": s, "adapt": 2 * (1 - x) + c}

    def remote(source, target, send, recv, device):
        return pltpu.make_async_remote_copy(
            src_ref=source, dst_ref=target, send_sem=send, recv_sem=recv,
            device_id=device, device_id_type=pl.DeviceIdType.MESH,
        )

    barrier = pltpu.get_barrier_semaphore()
    for k in range(1, 16):
        other = lax.rem(me + k, 16)
        pl.semaphore_signal(
            barrier, inc=1, device_id={"seq": other // 4, "adapt": lax.rem(other, 4)},
            device_id_type=pl.DeviceIdType.MESH,
        )
    pl.semaphore_wait(barrier, 15)

    for j in range(2):
        for h in range(2):
            place = 2 * c + j
            mine = jnp.logical_and(place == s, c == h)
            source, target = mod.at[j, h], tok.at[x, s, h]
            send, recv = tok_send.at[2 * j + h], tok_recv.at[s]

            @pl.when(mine)
            def _():
                pltpu.make_async_copy(source, target, recv).start()

            @pl.when(jnp.logical_not(mine))
            def _():
                remote(source, target, send, recv, {"seq": place, "adapt": 2 * x + h}).start()

    own = (
        pltpu.make_async_copy(down.at[:, s], down_all.at[a, s], down_recv.at[s]),
        pltpu.make_async_copy(up.at[:, s], up_all.at[s], up_recv.at[s]),
        pltpu.make_async_copy(text.at[:, s], txt.at[:, s], text_recv.at[s]),
    )
    for copy in own:
        copy.start()
    for k in range(1, 4):
        place = flipped(s, k)
        to = {"seq": place, "adapt": a}
        remote(down.at[:, place], down_all.at[a, s], down_send.at[k], down_recv.at[s], to).start()
        remote(up.at[:, place], up_all.at[s], up_send.at[k], up_recv.at[s], to).start()
        remote(text.at[:, place], txt.at[:, s], text_send.at[k], text_recv.at[s], to).start()

    def piece(k):
        return tok.at[x, flipped(s, k), c]

    def far_piece(k):
        return tok.at[1 - x, flipped(s, k), c]

    def first(k):
        return remote(piece(k), piece(k), tok_send.at[0], tok_recv.at[flipped(s, k)], sibling)

    def side(k):
        return remote(piece(k), piece(k), side_send.at[k], side_recv.at[k], sibling)

    def across(k):
        return remote(piece(k), piece(k), across_send.at[k], across_recv.at[k], partner)

    def across_in(k):
        return remote(far_piece(k), far_piece(k), across_send.at[k], across_recv.at[k], partner)

    def last(k):
        return remote(far_piece(k), far_piece(k), last_send.at[k], last_recv.at[k], sibling)

    def side_in(k):
        there = tok.at[x, flipped(s, k), 1 - c]
        return remote(there, there, side_send.at[k], side_recv.at[k], sibling)

    def last_in(k):
        there = tok.at[1 - x, flipped(s, k), 1 - c]
        return remote(there, there, last_send.at[k], last_recv.at[k], sibling)

    for k in range(4):
        first(k).wait_recv()
        across(k).start()
        side(k).start()
        if k > 0:
            across_in(k - 1).wait_recv()
            last(k - 1).start()
    for k in range(4):
        place = flipped(s, k)
        remote(
            down_all.at[a, place], down_all.at[a, place], down_send.at[0], down_recv.at[place], sibling
        ).wait_recv()
    for k in range(1, 4):
        remote(
            down_all.at[a], down_all.at[a], spread_send.at[k], spread_recv.at[k],
            {"seq": s, "adapt": flipped(a, k)},
        ).start()
    across_in(3).wait_recv()
    last(3).start()

    for j in range(2):
        for h in range(2):
            mine = jnp.logical_and(2 * c + j == s, c == h)

            @pl.when(jnp.logical_not(mine))
            def _():
                remote(
                    mod.at[j, h], tok.at[x, s, h], tok_send.at[2 * j + h], tok_recv.at[s], sibling
                ).wait_send()

    for k in range(4):
        side_in(k).wait_recv()
        last_in(k).wait_recv()
        side(k).wait_send()
        across(k).wait_send()
        last(k).wait_send()
        place = flipped(s, k)
        remote(up_all.at[place], up_all.at[place], up_send.at[0], up_recv.at[place], sibling).wait_recv()
        remote(
            txt.at[:, place], txt.at[:, place], text_send.at[0], text_recv.at[place], sibling
        ).wait_recv()
        if k > 0:
            remote(down.at[:, place], down_all.at[a, s], down_send.at[k], down_recv.at[s], sibling).wait_send()
            remote(up.at[:, place], up_all.at[s], up_send.at[k], up_recv.at[s], sibling).wait_send()
            remote(text.at[:, place], txt.at[:, s], text_send.at[k], text_recv.at[s], sibling).wait_send()
            other = flipped(a, k)
            remote(
                down_all.at[other], down_all.at[other], spread_send.at[k], spread_recv.at[k], sibling
            ).wait_recv()
            remote(
                down_all.at[a], down_all.at[a], spread_send.at[k], spread_recv.at[k], sibling
            ).wait_send()


def project_kernel(tok, weight, down, up, gain, q_out, k_out, v_out):
    rows = tok[0]
    shrunk = lax.dot_general(
        rows, down[0], (((1,), (1,)), ((), ())), preferred_element_type=F32
    ).astype(BF16)
    wide = 6 * HEAD_SIZE
    for part in range(weight.shape[1] // wide):
        columns = slice(part * wide, (part + 1) * wide)
        qkv = jnp.dot(rows, weight[:, columns], preferred_element_type=F32)
        qkv = qkv + jnp.dot(shrunk, up[0, :, columns], preferred_element_type=F32)
        for h in range(2):
            head = slice((2 * part + h) * HEAD_SIZE, (2 * part + h + 1) * HEAD_SIZE)
            q, k, v = (
                qkv[:, (3 * h + n) * HEAD_SIZE : (3 * h + n + 1) * HEAD_SIZE] for n in range(3)
            )
            q_out[0, :, head] = rms_scale(q, gain[0:1, :]).astype(BF16)
            k_out[0, :, head] = rms_scale(k, gain[1:2, :]).astype(BF16)
            v_out[0, :, head] = v.astype(BF16)


def attend_kernel(rows_at_once, q, k, v, txt, out, held, send, recv):
    s = lax.axis_index("seq")
    a = lax.axis_index("adapt")
    i = pl.program_id(0)
    token_local = held.shape[1]
    width = held.shape[2]
    factor = math.log2(math.e) / math.sqrt(HEAD_SIZE)

    @pl.when(i == 0)
    def _():
        barrier = pltpu.get_barrier_semaphore()
        for n in range(1, 4):
            pl.semaphore_signal(
                barrier, inc=1, device_id={"seq": flipped(s, n), "adapt": a},
                device_id_type=pl.DeviceIdType.MESH,
            )
        pl.semaphore_wait(barrier, 3)

    def remote(slot, row, sent, received, place):
        return pltpu.make_async_remote_copy(
            src_ref=held.at[slot], dst_ref=out.at[row], send_sem=send.at[sent],
            recv_sem=recv.at[received], device_id={"seq": place, "adapt": a},
            device_id_type=pl.DeviceIdType.MESH,
        )

    def one_block(step, carry):
        place = jnp.where(step == 3, s, jnp.where(step == 2, flipped(s, 1), jnp.where(step == 1, flipped(s, 3), flipped(s, 2))))
        slot = i * 4 + step
        for part in range(token_local // rows_at_once):
            rows = pl.ds(pl.multiple_of(place * token_local + part * rows_at_once, rows_at_once), rows_at_once)
            for h in range(width // HEAD_SIZE):
                head = slice(h * HEAD_SIZE, (h + 1) * HEAD_SIZE)
                value_head = slice(width + h * HEAD_SIZE, width + (h + 1) * HEAD_SIZE)
                queries = q[0, rows, head]
                over_last = (((1,), (1,)), ((), ()))
                first = lax.dot_general(queries, k[0, :, head], over_last, preferred_element_type=F32)
                second = lax.dot_general(queries, txt[0, :, head], over_last, preferred_element_type=F32)
                highest = jnp.maximum(
                    jnp.max(first, axis=-1, keepdims=True), jnp.max(second, axis=-1, keepdims=True)
                )
                first = jnp.exp2((first - highest) * factor)
                second = jnp.exp2((second - highest) * factor)
                share = 1.0 / (
                    jnp.sum(first, axis=-1, keepdims=True) + jnp.sum(second, axis=-1, keepdims=True)
                )
                total = jnp.dot((first * share).astype(BF16), v[0, :, head], preferred_element_type=F32)
                total = total + jnp.dot(
                    (second * share).astype(BF16), txt[0, :, value_head], preferred_element_type=F32
                )
                held[slot, part * rows_at_once : (part + 1) * rows_at_once, head] = total.astype(BF16)

        @pl.when(step == 3)
        def _():
            pltpu.make_async_copy(held.at[slot], out.at[i * 4 + s], recv.at[slot]).start()

        @pl.when(step < 3)
        def _():
            remote(slot, i * 4 + s, slot, slot, place).start()

        return carry

    lax.fori_loop(0, 4, one_block, 0)

    @pl.when(i == 1)
    def _():
        for row in range(2):
            for step, n in enumerate((2, 3, 1)):
                slot = row * 4 + step
                remote(slot, row * 4 + flipped(s, n), slot, slot, flipped(s, n)).wait()
            slot = row * 4 + 3
            pltpu.make_async_copy(held.at[slot], out.at[row * 4 + s], recv.at[slot]).wait()


def on_device(
    image,
    modulation,
    query_key_value_weight,
    pooled_down_factor,
    pooled_up_factor,
    request_adapter,
    adapter_slot_table,
    row_request,
    text_key_value,
    query_key_gain,
):
    seq_index = lax.axis_index("seq")
    all_requests = request_adapter.shape[0]
    pool_local, width, rank = pooled_down_factor.shape
    pool_total = adapter_slot_table.shape[0]
    columns = query_key_value_weight.shape[1]
    head_columns = columns // 3
    text_local = text_key_value.shape[1]
    token_local = image.shape[1]
    tokens = 4 * token_local
    modulated = layer_modulate(image, modulation)
    request_match = row_request[:, None] == jnp.arange(all_requests, dtype=jnp.int32)[None, :]
    chosen_ids = jnp.sum(jnp.where(request_match, request_adapter[None, :], 0), axis=1)
    slot_match = chosen_ids[:, None] == jnp.arange(pool_total, dtype=jnp.int32)[None, :]
    slots = jnp.sum(jnp.where(slot_match, adapter_slot_table[None, :], 0), axis=1)
    owned = slots // pool_local == seq_index
    local_match = (slots % pool_local)[:, None] == jnp.arange(pool_local, dtype=jnp.int32)[None, :]
    slot_picker = (owned[:, None] & local_match).astype(BF16)
    share = width // 4
    down_part = lax.dynamic_slice_in_dim(
        pooled_down_factor, lax.axis_index("adapt") * share, share, axis=1
    )
    down_terms = jnp.einsum(
        "mv,vna->man", slot_picker, down_part, preferred_element_type=F32
    ).astype(BF16)
    up_terms = jnp.einsum(
        "eq,qfx->efx", slot_picker, pooled_up_factor, preferred_element_type=F32
    ).astype(BF16)

    dma = pltpu.SemaphoreType.DMA((4,))
    tok, txt, down_all, up_all = pl.pallas_call(
        move_kernel,
        out_shape=(
            jax.ShapeDtypeStruct((2, 4, 2, token_local // 2, width), BF16),
            jax.ShapeDtypeStruct((2, 4, text_local, 2 * head_columns), BF16),
            jax.ShapeDtypeStruct((4, 4, 2, rank, share), BF16),
            jax.ShapeDtypeStruct((4, 2, rank, columns), BF16),
        ),
        in_specs=[ANY] * 4,
        out_specs=(ANY,) * 4,
        scratch_shapes=[dma] * 16,
        compiler_params=pltpu.CompilerParams(collective_id=0, has_side_effects=True),
        name="move_tokens",
    )(
        modulated.reshape(2, 2, token_local // 2, width),
        text_key_value.reshape(2, 4, text_local, 2 * head_columns),
        down_terms.reshape(2, 4, rank, share),
        up_terms.reshape(2, 4, rank, columns),
    )
    tok = tok.reshape(2, tokens, width)
    txt = txt.reshape(2, 4 * text_local, 2 * head_columns)
    down = jnp.sum(down_all.astype(F32), axis=1).astype(BF16)
    down = jnp.transpose(down, (1, 2, 0, 3)).reshape(2, rank, width)
    up = jnp.sum(up_all.astype(F32), axis=0).astype(BF16)

    block = token_local
    taken = jax.ShapeDtypeStruct((2, tokens, head_columns), BF16)
    block_spec = pl.BlockSpec((1, block, head_columns), lambda r, t: (r, t, 0))
    queries, keys, values = pl.pallas_call(
        project_kernel,
        out_shape=(taken,) * 3,
        grid=(2, tokens // block),
        in_specs=[
            pl.BlockSpec((1, block, width), lambda r, t: (r, t, 0)),
            pl.BlockSpec((width, columns), lambda r, t: (0, 0)),
            pl.BlockSpec((1, rank, width), lambda r, t: (r, 0, 0)),
            pl.BlockSpec((1, rank, columns), lambda r, t: (r, 0, 0)),
            pl.BlockSpec((2, HEAD_SIZE), lambda r, t: (0, 0)),
        ],
        out_specs=(block_spec,) * 3,
        compiler_params=pltpu.CompilerParams(vmem_limit_bytes=56 * 2**20),
        name="project",
    )(tok, query_key_value_weight, down, up, query_key_gain)

    whole_spec = pl.BlockSpec((1, tokens, head_columns), lambda r: (r, 0, 0))
    return pl.pallas_call(
        functools.partial(attend_kernel, min(256, token_local)),
        out_shape=jax.ShapeDtypeStruct((all_requests, token_local, head_columns), BF16),
        grid=(2,),
        in_specs=[whole_spec] * 3
        + [pl.BlockSpec((1, 4 * text_local, 2 * head_columns), lambda r: (r, 0, 0))],
        out_specs=ANY,
        scratch_shapes=[
            pltpu.VMEM((8, token_local, head_columns), BF16),
            pltpu.SemaphoreType.DMA((8,)),
            pltpu.SemaphoreType.DMA((8,)),
        ],
        compiler_params=pltpu.CompilerParams(
            collective_id=1, has_side_effects=True, vmem_limit_bytes=56 * 2**20
        ),
        name="attend",
    )(queries, keys, values, txt)


def solution(mesh):
    in_specs = (
        P(("groups", "adapt"), "seq", None),
        P(("groups", "adapt"), None, None),
        P(None, "adapt"),
        P("seq", None, None),
        P("seq", None, "adapt"),
        P("groups"),
        P(),
        P("groups"),
        P("groups", "seq", None, "adapt"),
        P(),
    )
    out_specs = P("groups", "seq", "adapt")
    def chosen(*operands):
        image, request_adapter = operands[0], operands[5]
        fits = (
            mesh.shape["seq"] == 4
            and mesh.shape["adapt"] == 4
            and request_adapter.shape[0] == 8
            and image.shape[0] == 2
            and operands[2].shape[1] % (6 * HEAD_SIZE) == 0
            and image.shape[1] % 256 == 0
            and image.shape[2] % 512 == 0
        )
        return (on_device if fits else general_device)(*operands)

    return jax.shard_map(
        chosen, mesh=mesh, in_specs=in_specs, out_specs=out_specs, check_vma=False
    )
```

```python
import functools
import math

import jax
import jax.numpy as jnp
from jax import lax
from jax.experimental import pallas as pl
from jax.experimental.pallas import tpu as pltpu
from jax.sharding import PartitionSpec as P

HEAD_SIZE = 128


def layer_modulate(image, modulation):
    widened = image.astype(jnp.float32)
    centre = widened - jnp.mean(widened, axis=-1, keepdims=True)
    variance = jnp.mean(centre * centre, axis=-1, keepdims=True)
    normed = centre * lax.rsqrt(variance + 1e-06)
    return ((1.0 + modulation[:, 1, None, :]) * normed + modulation[:, 0, None, :]).astype(
        jnp.bfloat16
    )


def rms_scale(values, gain):
    return values * lax.rsqrt(jnp.mean(values * values, axis=-1, keepdims=True) + 1e-06) * gain


def attend_item(operands):
    queries, joined = operands
    key_rows = joined[:, 0]
    value_rows = joined[:, 1]
    query_count = queries.shape[0]
    block = math.gcd(query_count, 512)
    inverse = 1.0 / math.sqrt(queries.shape[-1])
    blocked = queries.reshape(query_count // block, block, queries.shape[-1])

    def one_block(block_rows):
        scores = (
            lax.dot_general(
                block_rows, key_rows, (((1,), (1,)), ((), ())), preferred_element_type=jnp.float32
            )
            * inverse
        )
        highest = jnp.max(scores, axis=-1, keepdims=True)
        weights = jnp.exp(scores - highest)
        weights = weights / jnp.sum(weights, axis=-1, keepdims=True)
        return jnp.dot(
            weights.astype(jnp.bfloat16), value_rows, preferred_element_type=jnp.float32
        ).astype(jnp.bfloat16)

    return lax.map(one_block, blocked).reshape(queries.shape)


def general_device(
    image,
    modulation,
    query_key_value_weight,
    pooled_down_factor,
    pooled_up_factor,
    request_adapter,
    adapter_slot_table,
    row_request,
    text_key_value,
    query_key_gain,
):
    seq_index = lax.axis_index("seq")
    all_requests = request_adapter.shape[0]
    local_pool_slice = pooled_down_factor.shape[0]
    pool_total = adapter_slot_table.shape[0]
    heads_local = query_key_value_weight.shape[1] // (3 * HEAD_SIZE)
    text_local = text_key_value.shape[1]
    modulated = layer_modulate(image, modulation)
    request_match = row_request[:, None] == jnp.arange(all_requests, dtype=jnp.int32)[None, :]
    chosen_ids = jnp.sum(jnp.where(request_match, request_adapter[None, :], 0), axis=1)
    slot_match = chosen_ids[:, None] == jnp.arange(pool_total, dtype=jnp.int32)[None, :]
    slots = jnp.sum(jnp.where(slot_match, adapter_slot_table[None, :], 0), axis=1)
    owned = slots // local_pool_slice == seq_index
    local_match = (slots % local_pool_slice)[:, None] == jnp.arange(
        local_pool_slice, dtype=jnp.int32
    )[None, :]
    slot_picker = (owned[:, None] & local_match).astype(jnp.bfloat16)
    up_terms = jnp.einsum(
        "eq,qfx->efx", slot_picker, pooled_up_factor, preferred_element_type=jnp.float32
    ).astype(jnp.bfloat16)
    down_terms = jnp.einsum(
        "mv,vna->mna", slot_picker, pooled_down_factor, preferred_element_type=jnp.float32
    ).astype(jnp.bfloat16)
    down_fetched, up_fetched = (
        lax.psum(down_terms, "seq").astype(jnp.float32),
        lax.psum(up_terms, "seq").astype(jnp.float32),
    )
    down_fetched = down_fetched.astype(jnp.bfloat16)
    up_fetched = up_fetched.astype(jnp.bfloat16)
    block_rows = lax.all_gather(modulated, "adapt", axis=0, tiled=True)
    shrunk = jnp.einsum(
        "rtd,rdk->rtk", block_rows, down_fetched, preferred_element_type=jnp.float32
    ).astype(jnp.bfloat16)
    frozen = jnp.einsum(
        "rtd,dc->rtc", block_rows, query_key_value_weight, preferred_element_type=jnp.float32
    )
    qkv = frozen + jnp.einsum(
        "rtk,rkc->rtc", shrunk, up_fetched, preferred_element_type=jnp.float32
    )
    token_local = qkv.shape[1]
    qkv = qkv.reshape(all_requests, token_local, heads_local, 3, HEAD_SIZE)
    queries = rms_scale(qkv[:, :, :, 0], query_key_gain[0]).astype(jnp.bfloat16)
    image_keys = rms_scale(qkv[:, :, :, 1], query_key_gain[1]).astype(jnp.bfloat16)
    image_values = qkv[:, :, :, 2].astype(jnp.bfloat16)
    image_pairs = jnp.transpose(jnp.stack([image_keys, image_values], axis=3), (0, 2, 1, 3, 4))
    text_pairs = jnp.transpose(
        text_key_value.reshape(all_requests, text_local, 2, heads_local, HEAD_SIZE), (0, 3, 1, 2, 4)
    )
    joined = jnp.concatenate([image_pairs, text_pairs], axis=2)
    joined = joined.reshape(all_requests * heads_local, token_local + text_local, 2, HEAD_SIZE)
    queries = jnp.transpose(queries, (0, 2, 1, 3)).reshape(
        all_requests * heads_local, token_local, HEAD_SIZE
    )
    query_items, joined_items = (
        lax.all_to_all(queries, "seq", split_axis=0, concat_axis=1, tiled=True),
        lax.all_to_all(joined, "seq", split_axis=0, concat_axis=1, tiled=True),
    )
    attended = lax.map(attend_item, (query_items, joined_items))
    returned = lax.all_to_all(attended, "seq", split_axis=1, concat_axis=0, tiled=True)
    returned = returned.reshape(all_requests, heads_local, token_local, HEAD_SIZE)
    return jnp.transpose(returned, (0, 2, 1, 3)).reshape(
        all_requests, token_local, heads_local * HEAD_SIZE
    )


BF16 = jnp.bfloat16
ROUNDS = 4
F32 = jnp.float32
ANY = pl.BlockSpec(memory_space=pl.ANY)


def flipped(index, k):
    low = 1 - 2 * lax.rem(index, 2) if k % 2 else 0
    high = 2 - 4 * (index // 2) if k // 2 else 0
    return index + low + high


def move_kernel(
    mod, down, up, tok, down_all, up_all,
    tok_send, tok_recv, side_send, side_recv, across_send, across_recv, last_send, last_recv,
    up_send, up_recv, down_send, down_recv, spread_send, spread_recv,
):
    s = lax.axis_index("seq")
    a = lax.axis_index("adapt")
    x = a // 2
    c = lax.rem(a, 2)
    me = s * 4 + a
    sibling = {"seq": s, "adapt": 2 * x + 1 - c}
    partner = {"seq": s, "adapt": 2 * (1 - x) + c}

    def remote(source, target, send, recv, device):
        return pltpu.make_async_remote_copy(
            src_ref=source, dst_ref=target, send_sem=send, recv_sem=recv,
            device_id=device, device_id_type=pl.DeviceIdType.MESH,
        )

    barrier = pltpu.get_barrier_semaphore()
    for k in range(1, 16):
        other = lax.rem(me + k, 16)
        pl.semaphore_signal(
            barrier, inc=1, device_id={"seq": other // 4, "adapt": lax.rem(other, 4)},
            device_id_type=pl.DeviceIdType.MESH,
        )
    pl.semaphore_wait(barrier, 15)

    def handed(n, j, h):
        place = 2 * c + j
        mine = jnp.logical_and(place == s, c == h)
        recv = tok_recv.at[n, s]
        source, target = mod.at[j, h, n], tok.at[x, s, h, n]
        away = remote(
            source, target, tok_send.at[n, 2 * j + h], recv, {"seq": place, "adapt": 2 * x + h}
        )
        return mine, away, pltpu.make_async_copy(source, target, recv)

    def start_round(n):
        for j in range(2):
            for h in range(2):
                mine, away, here = handed(n, j, h)

                @pl.when(mine)
                def _():
                    here.start()

                @pl.when(jnp.logical_not(mine))
                def _():
                    away.start()

    def end_round(n):
        for j in range(2):
            for h in range(2):
                mine, away, _ = handed(n, j, h)

                @pl.when(jnp.logical_not(mine))
                def _():
                    away.wait_send()

    start_round(0)
    start_round(1)
    own = (
        pltpu.make_async_copy(down.at[:, s], down_all.at[a, s], down_recv.at[s]),
        pltpu.make_async_copy(up.at[:, s], up_all.at[s], up_recv.at[s]),
    )
    for copy in own:
        copy.start()
    for k in range(1, 4):
        place = flipped(s, k)
        to = {"seq": place, "adapt": a}
        remote(down.at[:, place], down_all.at[a, s], down_send.at[k], down_recv.at[s], to).start()
        remote(up.at[:, place], up_all.at[s], up_send.at[k], up_recv.at[s], to).start()

    def piece(n, k):
        return tok.at[x, flipped(s, k), c, n]

    def far_piece(n, k):
        return tok.at[1 - x, flipped(s, k), c, n]

    def first(n, k):
        return remote(piece(n, k), piece(n, k), tok_send.at[n, 0], tok_recv.at[n, flipped(s, k)], sibling)

    def side(n, k):
        return remote(piece(n, k), piece(n, k), side_send.at[n, k], side_recv.at[n, k], sibling)

    def across(n, k):
        return remote(piece(n, k), piece(n, k), across_send.at[n, k], across_recv.at[n, k], partner)

    def across_in(n, k):
        return remote(
            far_piece(n, k), far_piece(n, k), across_send.at[n, k], across_recv.at[n, k], partner
        )

    def last(n, k):
        return remote(far_piece(n, k), far_piece(n, k), last_send.at[n, k], last_recv.at[n, k], sibling)

    def side_in(n, k):
        there = tok.at[x, flipped(s, k), 1 - c, n]
        return remote(there, there, side_send.at[n, k], side_recv.at[n, k], sibling)

    def last_in(n, k):
        there = tok.at[1 - x, flipped(s, k), 1 - c, n]
        return remote(there, there, last_send.at[n, k], last_recv.at[n, k], sibling)

    for n in range(ROUNDS):
        for k in range(4):
            first(n, k).wait_recv()
            across(n, k).start()
            side(n, k).start()
        end_round(n)
        if n + 2 < ROUNDS:
            start_round(n + 2)
        if n > 0:
            for k in range(4):
                across_in(n - 1, k).wait_recv()
                last(n - 1, k).start()
    for k in range(4):
        place = flipped(s, k)
        remote(
            down_all.at[a, place], down_all.at[a, place], down_send.at[0], down_recv.at[place], sibling
        ).wait_recv()
    for k in range(1, 4):
        remote(
            down_all.at[a], down_all.at[a], spread_send.at[k], spread_recv.at[k],
            {"seq": s, "adapt": flipped(a, k)},
        ).start()
    for k in range(4):
        across_in(ROUNDS - 1, k).wait_recv()
        last(ROUNDS - 1, k).start()

    for k in range(4):
        for n in range(ROUNDS):
            side_in(n, k).wait_recv()
            last_in(n, k).wait_recv()
            side(n, k).wait_send()
            across(n, k).wait_send()
            last(n, k).wait_send()
        place = flipped(s, k)
        remote(up_all.at[place], up_all.at[place], up_send.at[0], up_recv.at[place], sibling).wait_recv()
        if k > 0:
            remote(down.at[:, place], down_all.at[a, s], down_send.at[k], down_recv.at[s], sibling).wait_send()
            remote(up.at[:, place], up_all.at[s], up_send.at[k], up_recv.at[s], sibling).wait_send()
            other = flipped(a, k)
            remote(
                down_all.at[other], down_all.at[other], spread_send.at[k], spread_recv.at[k], sibling
            ).wait_recv()
            remote(
                down_all.at[a], down_all.at[a], spread_send.at[k], spread_recv.at[k], sibling
            ).wait_send()


def project_kernel(
    tok, weight, down, up, gain, text, q_out, k_out, v_out, txt, text_send, text_recv
):
    s = lax.axis_index("seq")
    a = lax.axis_index("adapt")
    r = pl.program_id(0)
    t = pl.program_id(1)

    def text_copy(k):
        place = flipped(s, k)
        return pltpu.make_async_remote_copy(
            src_ref=text.at[:, place], dst_ref=txt.at[:, s], send_sem=text_send.at[k],
            recv_sem=text_recv.at[k], device_id={"seq": place, "adapt": a},
            device_id_type=pl.DeviceIdType.MESH,
        )

    own_text = pltpu.make_async_copy(text.at[:, s], txt.at[:, s], text_recv.at[0])

    @pl.when(jnp.logical_and(r == 0, t == 0))
    def _():
        barrier = pltpu.get_barrier_semaphore()
        for n in range(1, 4):
            pl.semaphore_signal(
                barrier, inc=1, device_id={"seq": flipped(s, n), "adapt": a},
                device_id_type=pl.DeviceIdType.MESH,
            )
        pl.semaphore_wait(barrier, 3)
        for k in (2, 3, 1):
            text_copy(k).start()
        own_text.start()

    rows = tok[0]
    shrunk = lax.dot_general(
        rows, down[0], (((1,), (1,)), ((), ())), preferred_element_type=F32
    ).astype(BF16)
    wide = 6 * HEAD_SIZE
    for part in range(weight.shape[1] // wide):
        columns = slice(part * wide, (part + 1) * wide)
        qkv = jnp.dot(rows, weight[:, columns], preferred_element_type=F32)
        qkv = qkv + jnp.dot(shrunk, up[0, :, columns], preferred_element_type=F32)
        for h in range(2):
            head = slice((2 * part + h) * HEAD_SIZE, (2 * part + h + 1) * HEAD_SIZE)
            q, k, v = (
                qkv[:, (3 * h + n) * HEAD_SIZE : (3 * h + n + 1) * HEAD_SIZE] for n in range(3)
            )
            q_out[0, :, head] = rms_scale(q, gain[0:1, :]).astype(BF16)
            k_out[0, :, head] = rms_scale(k, gain[1:2, :]).astype(BF16)
            v_out[0, :, head] = v.astype(BF16)

    @pl.when(jnp.logical_and(r == pl.num_programs(0) - 1, t == pl.num_programs(1) - 1))
    def _():
        for k in (2, 3, 1):
            text_copy(k).wait()
        own_text.wait()


def attend_kernel(rows_at_once, q, k, v, txt, out, held, send, recv):
    s = lax.axis_index("seq")
    a = lax.axis_index("adapt")
    i = pl.program_id(0)
    token_local = held.shape[1]
    width = held.shape[2]
    factor = math.log2(math.e) / math.sqrt(HEAD_SIZE)

    @pl.when(i == 0)
    def _():
        barrier = pltpu.get_barrier_semaphore()
        for n in range(1, 4):
            pl.semaphore_signal(
                barrier, inc=1, device_id={"seq": flipped(s, n), "adapt": a},
                device_id_type=pl.DeviceIdType.MESH,
            )
        pl.semaphore_wait(barrier, 3)

    def remote(slot, row, sent, received, place):
        return pltpu.make_async_remote_copy(
            src_ref=held.at[slot], dst_ref=out.at[row], send_sem=send.at[sent],
            recv_sem=recv.at[received], device_id={"seq": place, "adapt": a},
            device_id_type=pl.DeviceIdType.MESH,
        )

    def one_block(step, carry):
        place = jnp.where(step == 3, s, jnp.where(step == 2, flipped(s, 1), jnp.where(step == 1, flipped(s, 3), flipped(s, 2))))
        slot = i * 4 + step
        work = [
            (part, h) for part in range(token_local // rows_at_once) for h in range(width // HEAD_SIZE)
        ]

        def scores(part, h):
            rows = pl.ds(
                pl.multiple_of(place * token_local + part * rows_at_once, rows_at_once), rows_at_once
            )
            head = slice(h * HEAD_SIZE, (h + 1) * HEAD_SIZE)
            return tuple(
                lax.dot_general(
                    q[0, rows, head], key_rows, (((1,), (1,)), ((), ())), preferred_element_type=F32
                )
                for key_rows in (k[0, :, head], txt[0, :, head])
            )

        ready = scores(*work[0])
        for n, (part, h) in enumerate(work):
            first, second = ready
            if n + 1 < len(work):
                ready = scores(*work[n + 1])
            head = slice(h * HEAD_SIZE, (h + 1) * HEAD_SIZE)
            value_head = slice(width + h * HEAD_SIZE, width + (h + 1) * HEAD_SIZE)
            highest = jnp.maximum(
                jnp.max(first, axis=-1, keepdims=True), jnp.max(second, axis=-1, keepdims=True)
            )
            first = jnp.exp2((first - highest) * factor)
            second = jnp.exp2((second - highest) * factor)
            share = 1.0 / (
                jnp.sum(first, axis=-1, keepdims=True) + jnp.sum(second, axis=-1, keepdims=True)
            )
            total = jnp.dot((first * share).astype(BF16), v[0, :, head], preferred_element_type=F32)
            total = total + jnp.dot(
                (second * share).astype(BF16), txt[0, :, value_head], preferred_element_type=F32
            )
            held[slot, part * rows_at_once : (part + 1) * rows_at_once, head] = total.astype(BF16)

        @pl.when(step == 3)
        def _():
            pltpu.make_async_copy(held.at[slot], out.at[i * 4 + s], recv.at[slot]).start()

        @pl.when(step < 3)
        def _():
            remote(slot, i * 4 + s, slot, slot, place).start()

        return carry

    lax.fori_loop(0, 4, one_block, 0)

    @pl.when(i == 1)
    def _():
        for row in range(2):
            for step, n in enumerate((2, 3, 1)):
                slot = row * 4 + step
                remote(slot, row * 4 + flipped(s, n), slot, slot, flipped(s, n)).wait()
            slot = row * 4 + 3
            pltpu.make_async_copy(held.at[slot], out.at[row * 4 + s], recv.at[slot]).wait()


def on_device(
    image,
    modulation,
    query_key_value_weight,
    pooled_down_factor,
    pooled_up_factor,
    request_adapter,
    adapter_slot_table,
    row_request,
    text_key_value,
    query_key_gain,
):
    seq_index = lax.axis_index("seq")
    all_requests = request_adapter.shape[0]
    pool_local, width, rank = pooled_down_factor.shape
    pool_total = adapter_slot_table.shape[0]
    columns = query_key_value_weight.shape[1]
    head_columns = columns // 3
    text_local = text_key_value.shape[1]
    token_local = image.shape[1]
    tokens = 4 * token_local
    modulated = layer_modulate(image, modulation)
    request_match = row_request[:, None] == jnp.arange(all_requests, dtype=jnp.int32)[None, :]
    chosen_ids = jnp.sum(jnp.where(request_match, request_adapter[None, :], 0), axis=1)
    slot_match = chosen_ids[:, None] == jnp.arange(pool_total, dtype=jnp.int32)[None, :]
    slots = jnp.sum(jnp.where(slot_match, adapter_slot_table[None, :], 0), axis=1)
    owned = slots // pool_local == seq_index
    local_match = (slots % pool_local)[:, None] == jnp.arange(pool_local, dtype=jnp.int32)[None, :]
    slot_picker = (owned[:, None] & local_match).astype(BF16)
    share = width // 4
    down_part = lax.dynamic_slice_in_dim(
        pooled_down_factor, lax.axis_index("adapt") * share, share, axis=1
    )
    down_terms = jnp.einsum(
        "mv,vna->man", slot_picker, down_part, preferred_element_type=F32
    ).astype(BF16)
    up_terms = jnp.einsum(
        "eq,qfx->efx", slot_picker, pooled_up_factor, preferred_element_type=F32
    ).astype(BF16)

    dma = pltpu.SemaphoreType.DMA((4,))
    tok, down_all, up_all = pl.pallas_call(
        move_kernel,
        out_shape=(
            jax.ShapeDtypeStruct((2, 4, 2, ROUNDS, token_local // (2 * ROUNDS), width), BF16),
            jax.ShapeDtypeStruct((4, 4, 2, rank, share), BF16),
            jax.ShapeDtypeStruct((4, 2, rank, columns), BF16),
        ),
        in_specs=[ANY] * 3,
        out_specs=(ANY,) * 3,
        scratch_shapes=[pltpu.SemaphoreType.DMA((ROUNDS, 4))] * 8 + [dma] * 6,
        compiler_params=pltpu.CompilerParams(collective_id=0, has_side_effects=True),
        name="move_tokens",
    )(
        modulated.reshape(2, 2, ROUNDS, token_local // (2 * ROUNDS), width),
        down_terms.reshape(2, 4, rank, share),
        up_terms.reshape(2, 4, rank, columns),
    )
    tok = tok.reshape(2, tokens, width)
    down = jnp.sum(down_all.astype(F32), axis=1).astype(BF16)
    down = jnp.transpose(down, (1, 2, 0, 3)).reshape(2, rank, width)
    up = jnp.sum(up_all.astype(F32), axis=0).astype(BF16)

    block = token_local
    taken = jax.ShapeDtypeStruct((2, tokens, head_columns), BF16)
    block_spec = pl.BlockSpec((1, block, head_columns), lambda r, t: (r, t, 0))
    queries, keys, values, txt = pl.pallas_call(
        project_kernel,
        out_shape=(taken,) * 3
        + (jax.ShapeDtypeStruct((2, 4, text_local, 2 * head_columns), BF16),),
        grid=(2, tokens // block),
        in_specs=[
            pl.BlockSpec((1, block, width), lambda r, t: (r, t, 0)),
            pl.BlockSpec((width, columns), lambda r, t: (0, 0)),
            pl.BlockSpec((1, rank, width), lambda r, t: (r, 0, 0)),
            pl.BlockSpec((1, rank, columns), lambda r, t: (r, 0, 0)),
            pl.BlockSpec((2, HEAD_SIZE), lambda r, t: (0, 0)),
            ANY,
        ],
        out_specs=(block_spec,) * 3 + (ANY,),
        scratch_shapes=[dma] * 2,
        compiler_params=pltpu.CompilerParams(
            collective_id=2, has_side_effects=True, vmem_limit_bytes=56 * 2**20
        ),
        name="project",
    )(
        tok, query_key_value_weight, down, up, query_key_gain,
        text_key_value.reshape(2, 4, text_local, 2 * head_columns),
    )
    txt = txt.reshape(2, 4 * text_local, 2 * head_columns)

    whole_spec = pl.BlockSpec((1, tokens, head_columns), lambda r: (r, 0, 0))
    return pl.pallas_call(
        functools.partial(attend_kernel, math.gcd(512, token_local)),
        out_shape=jax.ShapeDtypeStruct((all_requests, token_local, head_columns), BF16),
        grid=(2,),
        in_specs=[whole_spec] * 3
        + [pl.BlockSpec((1, 4 * text_local, 2 * head_columns), lambda r: (r, 0, 0))],
        out_specs=ANY,
        scratch_shapes=[
            pltpu.VMEM((8, token_local, head_columns), BF16),
            pltpu.SemaphoreType.DMA((8,)),
            pltpu.SemaphoreType.DMA((8,)),
        ],
        compiler_params=pltpu.CompilerParams(
            collective_id=1, has_side_effects=True, vmem_limit_bytes=56 * 2**20
        ),
        name="attend",
    )(queries, keys, values, txt)


def solution(mesh):
    in_specs = (
        P(("groups", "adapt"), "seq", None),
        P(("groups", "adapt"), None, None),
        P(None, "adapt"),
        P("seq", None, None),
        P("seq", None, "adapt"),
        P("groups"),
        P(),
        P("groups"),
        P("groups", "seq", None, "adapt"),
        P(),
    )
    out_specs = P("groups", "seq", "adapt")
    def chosen(*operands):
        image, request_adapter = operands[0], operands[5]
        fits = (
            mesh.shape["seq"] == 4
            and mesh.shape["adapt"] == 4
            and request_adapter.shape[0] == 8
            and image.shape[0] == 2
            and operands[2].shape[1] % (6 * HEAD_SIZE) == 0
            and image.shape[1] % 256 == 0
            and image.shape[2] % 512 == 0
        )
        return (on_device if fits else general_device)(*operands)

    return jax.shard_map(
        chosen, mesh=mesh, in_specs=in_specs, out_specs=out_specs, check_vma=False
    )
```
